256 devices in a mesh: layer: 8 (over y, core), trace: 32 (over x, z).
Axes of the slice: x: 4, y: 4, z: 8, core: 2. Of those that a mesh axis runs over, the one named last changes fastest.
Arguments:
- source_up: bfloat16 [8, 32768, 256], P('layer', 'trace'), may hold values from -6 to 6
- source_down: bfloat16 [8, 32768, 256], P('layer', 'trace'), may hold values from -6 to 6
- diag_up: bfloat16 [8, 2, 32768, 1024], P('layer', None, 'trace'), may hold values from -0.125 to 0.125
- diag_down: bfloat16 [8, 2, 32768, 1024], P('layer', None, 'trace'), may hold values from -0.125 to 0.125
- projection: bfloat16 [8, 2, 32, 32768], P('layer', None, None, 'trace'), may hold values from -0.1875 to 0.1875
- expansion: bfloat16 [8, 2, 32, 32768], P('layer', None, None, 'trace'), may hold values from -1 to 1
- coupling: bfloat16 [8, 2, 2, 1024, 1024], P('layer', None, None, 'trace'), may hold values from -0.125 to 0.125
Outputs:
- trace_up: bfloat16 [8, 32768, 256], P('layer', 'trace')
- trace_down: bfloat16 [8, 32768, 256], P('layer', 'trace')
The draws below stay inside these ranges and needn't reach their ends.
All inputs are finite; a program needn't handle non-finite values.
Results may differ from the reference program's by a relative error of at most 0.013.
Values may be sent and summed in bfloat16 or wider, within the bound.
A program may use at most 64 MiB of HBM per device.

```python
import jax
import jax.numpy as jnp
from jax import lax

P_DEV = 1024
K = 32
SRC = 128
ITERS = 3
GROUPS = 8
POINTS = 32768
KTOT = 1024
N_TRACE = 32


def block_levels(own_key, extent, pieces, low, top_value):
    def one(position, shards_of):
        draws = jax.random.uniform(jax.random.fold_in(jax.random.fold_in(own_key, 6), position), (shards_of,), jnp.float32, low / len(pieces), top_value / len(pieces))
        return jnp.repeat(jnp.exp(draws), extent[position] // shards_of).reshape((-1,) + (1,) * (len(extent) - position - 1))

    gain = one(*pieces[0])
    for cut in pieces[1:]:
        gain = gain * one(*cut)
    return gain


def scatter_about(stream_key, shape, deviation, reach, pieces=(), dtype=jnp.bfloat16):
    level = block_levels(stream_key, shape, pieces, -0.22, 0.18) if pieces else 1.0
    values = jax.random.normal(stream_key, shape, jnp.float32) * deviation * level
    return jnp.minimum(jnp.maximum(values, -reach), reach).astype(dtype)


def setup_inputs(seed: int = 0) -> dict:
    streams_of = jax.random.split(jax.random.key(seed), 8)
    source_up = scatter_about(streams_of[0], (GROUPS, POINTS, 2 * SRC), 1.0, 6.0, ((0, 8), (1, 32)))
    source_down = scatter_about(streams_of[1], (GROUPS, POINTS, 2 * SRC), 1.0, 6.0, ((0, 8), (1, 32)))
    diag_up = scatter_about(streams_of[2], (GROUPS, 2, POINTS, P_DEV), (2 * P_DEV) ** -0.5, 0.125, ((0, 8), (2, 32)))
    diag_down = scatter_about(streams_of[3], (GROUPS, 2, POINTS, P_DEV), (2 * P_DEV) ** -0.5, 0.125, ((0, 8), (2, 32)))
    projection = scatter_about(streams_of[4], (GROUPS, 2, K, POINTS), P_DEV ** -0.5, 0.1875, ((0, 8), (3, 32)))
    expansion = scatter_about(streams_of[5], (GROUPS, 2, K, POINTS), K ** -0.5, 1.0, ((0, 8), (3, 32)))
    coupling = scatter_about(streams_of[6], (GROUPS, 2, 2, KTOT, KTOT), (2 * KTOT) ** -0.5, 0.125, ((0, 8), (3, 32)))
    return {"source_up": source_up, "source_down": source_down, "diag_up": diag_up, "diag_down": diag_down, "projection": projection, "expansion": expansion, "coupling": coupling}


def rotate(field):
    half = field.shape[-1] // 2
    return jnp.concatenate([-field[..., half:], field[..., :half]], axis=-1)


def layer_result(operands):
    field, block, basis_in, basis_out, couple = operands
    owners = N_TRACE
    values = field.astype(jnp.float32).reshape(owners, P_DEV, -1)
    proj = basis_in.astype(jnp.float32).reshape(K, owners, P_DEV)
    coeffs = jnp.einsum('kop,ops->oks', proj, values).reshape(owners * K, -1).astype(jnp.bfloat16)
    gathered = coeffs.astype(jnp.float32)
    coupled = jnp.dot(couple[0].astype(jnp.float32), gathered) + jnp.dot(couple[1].astype(jnp.float32), rotate(gathered))
    coupled = coupled.astype(jnp.bfloat16).astype(jnp.float32).reshape(owners, K, -1)
    expand = basis_out.astype(jnp.float32).reshape(K, owners, P_DEV)
    dense = block.astype(jnp.float32).reshape(2, owners, P_DEV, P_DEV)
    result = jnp.einsum('opq,oqs->ops', dense[0], values)
    result = result + jnp.einsum('opq,oqs->ops', dense[1], rotate(values))
    result = result + jnp.einsum('kop,oks->ops', expand, coupled)
    return result.reshape(owners * P_DEV, -1).astype(jnp.bfloat16)


def reference(source_up, source_down, diag_up, diag_down, projection, expansion, coupling):
    upward = source_up
    downward = source_down
    for step in range(ITERS):
        result_up = lax.map(layer_result, (upward, diag_up, projection[:, 0], expansion[:, 0], coupling[:, 0]))
        result_down = lax.map(layer_result, (downward, diag_down, projection[:, 1], expansion[:, 1], coupling[:, 1]))
        zeros = jnp.zeros_like(result_up[:1])
        arrived_up = jnp.concatenate([zeros, result_up[:-1]], axis=0)
        arrived_down = jnp.concatenate([result_down[1:], zeros], axis=0)
        upward = (source_up.astype(jnp.float32) + arrived_up.astype(jnp.float32)).astype(jnp.bfloat16)
        downward = (source_down.astype(jnp.float32) + arrived_down.astype(jnp.float32)).astype(jnp.bfloat16)
    return upward, downward
```

```python
import jax
import jax.numpy as jnp
from jax import lax
from jax.experimental import pallas as pl
from jax.experimental.pallas import tpu as pltpu
from jax.sharding import PartitionSpec as P

ITERS = 3
NX, NZ = 4, 8
CHUNKS = 4
MESH = pl.DeviceIdType.MESH


def combine(stacked):
    rows, half = stacked.shape[0] // 2, stacked.shape[1] // 2
    top, low = stacked[:rows], stacked[rows:]
    return jnp.concatenate([top[:, :half] - low[:, half:], top[:, half:] + low[:, :half]], axis=1)


def kernel(
    src_up, src_dn, dg_up, dg_dn, proj, expn, coup, out_up, out_dn,
    s_v, diag_v, proj_v, exp_v, etr, cblk, ag, bv, arr, psend, prec, v_v,
    ld, dld, c_s, c_r, e_s, e_r, ag_s, ag_r, bv_s, bv_r, p_s, p_r,
):
    g = lax.axis_index("layer")
    t = lax.axis_index("trace")
    layers = lax.axis_size("layer")
    x, z = lax.div(t, NZ), lax.rem(t, NZ)
    points, cols = s_v.shape[1:]
    k_own = proj_v.shape[1]
    kc = NZ * k_own
    rows = points // CHUNKS
    sends = (g < layers - 1, g > 0)
    takes = (g > 0, g < layers - 1)
    step = (1, -1)
    outs = (out_up, out_dn)

    def at(gg, xx, zz):
        return (gg, xx * NZ + zz)

    loads = [
        pltpu.make_async_copy(src_up.at[0], s_v.at[0], ld.at[0]),
        pltpu.make_async_copy(src_dn.at[0], s_v.at[1], ld.at[1]),
        pltpu.make_async_copy(proj.at[0], proj_v, ld.at[2]),
        pltpu.make_async_copy(
            coup.at[0, :, :, :, pl.ds(pl.multiple_of(x * kc, kc), kc)], cblk.at[:, x], ld.at[3]
        ),
    ]
    for copy in loads:
        copy.start()

    def diag_load(d, c):
        src = (dg_up, dg_dn)[d]
        return pltpu.make_async_copy(
            src.at[0, :, pl.ds(c * rows, rows), :], diag_v.at[d, c], dld.at[d, c]
        )

    for c in range(CHUNKS):
        for d in range(2):
            diag_load(d, c).start()

    barrier = pltpu.get_barrier_semaphore()
    for dz in range(1, NZ):
        pl.semaphore_signal(barrier, inc=1, device_id=at(g, x, lax.rem(z + dz, NZ)), device_id_type=MESH)
    for dx in range(1, NX):
        pl.semaphore_signal(barrier, inc=1, device_id=at(g, lax.rem(x + dx, NX), z), device_id_type=MESH)
    for d in range(2):
        @pl.when(sends[d])
        def _():
            for dx in range(NX):
                pl.semaphore_signal(
                    barrier, inc=1, device_id=at(g + step[d], lax.rem(x + dx, NX), z), device_id_type=MESH
                )

    loads[0].wait()
    loads[1].wait()
    loads[2].wait()
    zrow = pl.ds(pl.multiple_of(z * k_own, k_own), k_own)

    def coeffs(k, d, field):
        c = jnp.dot(proj_v[d], field[...], preferred_element_type=jnp.float32)
        ag[k, d, zrow, :] = c.astype(jnp.bfloat16)

    def gather_copy(k, d, dz):
        return pltpu.make_async_remote_copy(
            src_ref=ag.at[k, d, zrow, :],
            dst_ref=ag.at[k, d, zrow, :],
            send_sem=ag_s.at[k, d, dz - 1],
            recv_sem=ag_r.at[k, d, dz - 1],
            device_id=at(g, x, lax.rem(z + dz, NZ)),
            device_id_type=MESH,
        )

    far_first = sorted(range(1, NZ), key=lambda dz: -min(dz, NZ - dz))

    def gather_start(k, d):
        for dz in far_first:
            gather_copy(k, d, dz).start()

    for d in range(2):
        @pl.when(sends[d])
        def _():
            coeffs(0, d, s_v.at[d])

    ends = (g > 0).astype(jnp.int32) + (g < layers - 1).astype(jnp.int32)
    pl.semaphore_wait(barrier, NZ - 1 + NX - 1 + NX * ends)

    for d in range(2):
        @pl.when(sends[d])
        def _():
            gather_start(0, d)

    def coupling_copy(dx):
        to = lax.rem(x + dx, NX)
        return pltpu.make_async_remote_copy(
            src_ref=coup.at[0, :, :, :, pl.ds(pl.multiple_of(to * kc, kc), kc)],
            dst_ref=cblk.at[:, x],
            send_sem=c_s.at[dx - 1],
            recv_sem=c_r.at[dx - 1],
            device_id=at(g, to, z),
            device_id_type=MESH,
        )

    for dx in range(1, NX):
        coupling_copy(dx).start()

    def expansion_copy(d):
        return pltpu.make_async_remote_copy(
            src_ref=expn.at[0, d],
            dst_ref=exp_v.at[d],
            send_sem=e_s.at[d],
            recv_sem=e_r.at[d],
            device_id=at(g + step[d], x, z),
            device_id_type=MESH,
        )

    for d in range(2):
        @pl.when(sends[d])
        def _():
            expansion_copy(d).start()

    def dense_copy(k, d, c):
        part = pl.ds(pl.multiple_of(c * rows, rows), rows)
        return pltpu.make_async_remote_copy(
            src_ref=bv.at[k, d, part, :],
            dst_ref=arr.at[k, d, part, :],
            send_sem=bv_s.at[k, d, c],
            recv_sem=bv_r.at[k, d, c],
            device_id=at(g + step[d], x, z),
            device_id_type=MESH,
        )

    def partial_copy(k, d, dx):
        to = lax.rem(x + dx, NX)
        return pltpu.make_async_remote_copy(
            src_ref=psend.at[k, d, to],
            dst_ref=prec.at[k, d, x],
            send_sem=p_s.at[k, d, dx],
            recv_sem=p_r.at[k, d, dx],
            device_id=at(g + step[d], to, z),
            device_id_type=MESH,
        )

    def dense(k, d, c, field):
        part = pl.ds(pl.multiple_of(c * rows, rows), rows)
        both = diag_v[d, c].reshape(2 * rows, points)
        y = jnp.dot(both, field[...], preferred_element_type=jnp.float32)
        bv[k, d, part, :] = combine(y).astype(jnp.bfloat16)
        dense_copy(k, d, c).start()

    def couple(k, d):
        for dz in range(1, NZ):
            gather_copy(k, d, dz).wait_recv()
        gathered = ag[k, d]
        for to in range(NX):
            block = cblk[d, to].reshape(2 * k_own, kc)
            y = jnp.dot(block, gathered, preferred_element_type=jnp.float32)
            psend[k, d, to] = combine(y).astype(jnp.bfloat16)
        for dx in sorted(range(NX), key=lambda dx: -min(dx, NX - dx)):
            partial_copy(k, d, dx).start()

    def assemble(k, d, into):
        for dx in range(NX):
            partial_copy(k, d, dx).wait_recv()
        total = prec[k, d, 0].astype(jnp.float32)
        for xx in range(1, NX):
            total = total + prec[k, d, xx].astype(jnp.float32)
        coupled = total.astype(jnp.bfloat16)

        def one(c, carry):
            part = pl.ds(pl.multiple_of(c * rows, rows), rows)
            dense_copy(k, d, c).wait_recv()
            y = jnp.dot(etr[d, part, :], coupled, preferred_element_type=jnp.float32)
            y = y + arr[k, d, part, :].astype(jnp.float32) + s_v[d, part, :].astype(jnp.float32)
            into[part, :] = y.astype(jnp.bfloat16)
            return carry

        lax.fori_loop(0, CHUNKS, one, 0)

    for k in range(ITERS):
        fields = (s_v.at[0], s_v.at[1]) if k == 0 else (v_v.at[0], v_v.at[1])

        def chunk(c, carry):
            for d in range(2):
                if k == 0:
                    diag_load(d, c).wait()

                @pl.when(sends[d])
                def _():
                    dense(k, d, c, fields[d])

            return carry

        lax.fori_loop(0, CHUNKS, chunk, 0)
        if k == 0:
            loads[3].wait()
            for dx in range(1, NX):
                coupling_copy(dx).wait_recv()
            for d in range(2):
                @pl.when(takes[d])
                def _():
                    expansion_copy(d).wait_recv()
                    etr[d] = exp_v[d].astype(jnp.float32).T.astype(jnp.bfloat16)

        for d in range(2):
            @pl.when(sends[d])
            def _():
                couple(k, d)

        for d in range(2):
            into = outs[d].at[0] if k == ITERS - 1 else v_v.at[d]

            @pl.when(takes[d])
            def _():
                assemble(k, d, into)

            if k == ITERS - 1 or k == 0:
                @pl.when(jnp.logical_not(takes[d]))
                def _():
                    into[...] = s_v[d]

            if k < ITERS - 1:
                @pl.when(sends[d])
                def _():
                    coeffs(k + 1, d, v_v.at[d])
                    gather_start(k + 1, d)

    for dx in range(1, NX):
        coupling_copy(dx).wait_send()
    for d in range(2):
        @pl.when(sends[d])
        def _():
            expansion_copy(d).wait_send()
            for k in range(ITERS):
                for dz in range(1, NZ):
                    gather_copy(k, d, dz).wait_send()
                for c in range(CHUNKS):
                    dense_copy(k, d, c).wait_send()
                for dx in range(NX):
                    partial_copy(k, d, dx).wait_send()


def shards(source_up, source_down, diag_up, diag_down, projection, expansion, coupling):
    points, cols = source_up.shape[1:]
    k_own = projection.shape[2]
    kc = NZ * k_own
    rows = points // CHUNKS
    bf = jnp.bfloat16
    sem = pltpu.SemaphoreType.DMA
    hbm = pl.BlockSpec(memory_space=pl.ANY)
    vmem = pl.BlockSpec(memory_space=pltpu.VMEM)
    return pl.pallas_call(
        kernel,
        out_shape=(
            jax.ShapeDtypeStruct(source_up.shape, bf),
            jax.ShapeDtypeStruct(source_down.shape, bf),
        ),
        in_specs=[hbm] * 7,
        out_specs=(vmem, vmem),
        scratch_shapes=[
            pltpu.VMEM((2, points, cols), bf),
            pltpu.VMEM((2, CHUNKS, 2, rows, points), bf),
            pltpu.VMEM((2, k_own, points), bf),
            pltpu.VMEM((2, k_own, points), bf),
            pltpu.VMEM((2, points, k_own), bf),
            pltpu.VMEM((2, NX, 2, k_own, kc), bf),
            pltpu.VMEM((ITERS, 2, kc, cols), bf),
            pltpu.VMEM((ITERS, 2, points, cols), bf),
            pltpu.VMEM((ITERS, 2, points, cols), bf),
            pltpu.VMEM((ITERS, 2, NX, k_own, cols), bf),
            pltpu.VMEM((ITERS, 2, NX, k_own, cols), bf),
            pltpu.VMEM((2, points, cols), bf),
            sem((4,)),
            sem((2, CHUNKS)),
            sem((NX - 1,)),
            sem((NX - 1,)),
            sem((2,)),
            sem((2,)),
            sem((ITERS, 2, NZ - 1)),
            sem((ITERS, 2, NZ - 1)),
            sem((ITERS, 2, CHUNKS)),
            sem((ITERS, 2, CHUNKS)),
            sem((ITERS, 2, NX)),
            sem((ITERS, 2, NX)),
        ],
        compiler_params=pltpu.CompilerParams(
            collective_id=0, has_side_effects=True, vmem_limit_bytes=60 * 1024 * 1024
        ),
        name="traces",
    )(source_up, source_down, diag_up, diag_down, projection, expansion, coupling)


def solution(mesh):
    return jax.shard_map(
        shards,
        mesh=mesh,
        in_specs=(
            P("layer", "trace", None),
            P("layer", "trace", None),
            P("layer", None, "trace", None),
            P("layer", None, "trace", None),
            P("layer", None, None, "trace"),
            P("layer", None, None, "trace"),
            P("layer", None, None, "trace", None),
        ),
        out_specs=(P("layer", "trace", None), P("layer", "trace", None)),
        check_vma=False,
    )
```

```python
import jax
import jax.numpy as jnp
from jax import lax
from jax.experimental import pallas as pl
from jax.experimental.pallas import tpu as pltpu
from jax.sharding import PartitionSpec as P

ITERS = 3
NX, NZ = 4, 8
CHUNKS = 4
MESH = pl.DeviceIdType.MESH


def combine(stacked):
    rows, half = stacked.shape[0] // 2, stacked.shape[1] // 2
    top, low = stacked[:rows], stacked[rows:]
    return jnp.concatenate([top[:, :half] - low[:, half:], top[:, half:] + low[:, :half]], axis=1)


def kernel(
    src_up, src_dn, dg_up, dg_dn, proj, expn, coup, out,
    s_v, diag_v, proj_v, exp_v, etr, small, base, cblk, ag, bv, arr, psend, prec, cpl, v_v,
    ld, dld, c_s, c_r, e_s, e_r, ag_s, ag_r, bv_s, bv_r, p_s, p_r,
):
    g = lax.axis_index("layer")
    t = lax.axis_index("trace")
    layers = lax.axis_size("layer")
    x, z = lax.div(t, NZ), lax.rem(t, NZ)
    points, cols = s_v.shape[1:]
    k_own = proj_v.shape[1]
    kc = NZ * k_own
    rows = points // CHUNKS
    first, second = 0, 1
    order = (first, second)
    f32, bf16 = jnp.float32, jnp.bfloat16

    def at(gg, xx, zz):
        return (gg, xx * NZ + zz)

    def ahead(d):
        return g + 1 - 2 * d

    def sends(d):
        return jnp.logical_and(ahead(d) >= 0, ahead(d) < layers)

    def takes(d):
        behind = g - 1 + 2 * d
        return jnp.logical_and(behind >= 0, behind < layers)

    loads = [
        pltpu.make_async_copy(proj.at[0], proj_v, ld.at[2]),
        pltpu.make_async_copy(src_up.at[0], s_v.at[0], ld.at[0]),
        pltpu.make_async_copy(src_dn.at[0], s_v.at[1], ld.at[1]),
        pltpu.make_async_copy(
            coup.at[0, :, :, :, pl.ds(pl.multiple_of(x * kc, kc), kc)], cblk.at[:, x], ld.at[3]
        ),
    ]
    for copy in loads:
        copy.start()

    barrier = pltpu.get_barrier_semaphore()
    for dz in range(1, NZ):
        pl.semaphore_signal(barrier, inc=1, device_id=at(g, x, lax.rem(z + dz, NZ)), device_id_type=MESH)
    for dx in range(1, NX):
        pl.semaphore_signal(barrier, inc=1, device_id=at(g, lax.rem(x + dx, NX), z), device_id_type=MESH)
    for d in range(2):
        @pl.when(sends(d))
        def _():
            for dx in range(NX):
                pl.semaphore_signal(
                    barrier, inc=1, device_id=at(ahead(d), lax.rem(x + dx, NX), z), device_id_type=MESH
                )

    def diag_load(d, c):
        src = (dg_up, dg_dn)[d]
        return pltpu.make_async_copy(
            src.at[0, :, pl.ds(c * rows, rows), :], diag_v.at[d, c], dld.at[d, c]
        )

    def diag_start(d):
        for c in range(CHUNKS):
            diag_load(d, c).start()

    diag_start(0)
    diag_start(1)

    for copy in loads[:3]:
        copy.wait()
    zrow = pl.ds(pl.multiple_of(z * k_own, k_own), k_own)

    def gather_copy(k, d, dz):
        return pltpu.make_async_remote_copy(
            src_ref=ag.at[k, d, zrow, :],
            dst_ref=ag.at[k, d, zrow, :],
            send_sem=ag_s.at[k, d, dz - 1],
            recv_sem=ag_r.at[k, d, dz - 1],
            device_id=at(g, x, lax.rem(z + dz, NZ)),
            device_id_type=MESH,
        )

    def far_first(count, start):
        return sorted(range(start, count), key=lambda step: -min(step, count - step))

    def gather_start(k, d):
        for dz in far_first(NZ, 1):
            gather_copy(k, d, dz).start()

    for d in range(2):
        @pl.when(sends(d))
        def _():
            c = jnp.dot(proj_v[d], s_v[d], preferred_element_type=f32)
            ag[0, d, zrow, :] = c.astype(bf16)

        @pl.when(jnp.logical_not(takes(d)))
        def _():
            v_v[d] = s_v[d]

    ends = (g > 0).astype(jnp.int32) + (g < layers - 1).astype(jnp.int32)
    pl.semaphore_wait(barrier, NZ - 1 + NX - 1 + NX * ends)

    for d in order:
        @pl.when(sends(d))
        def _():
            gather_start(0, d)

    def coupling_copy(dx):
        to = lax.rem(x + dx, NX)
        return pltpu.make_async_remote_copy(
            src_ref=coup.at[0, :, :, :, pl.ds(pl.multiple_of(to * kc, kc), kc)],
            dst_ref=cblk.at[:, x],
            send_sem=c_s.at[dx - 1],
            recv_sem=c_r.at[dx - 1],
            device_id=at(g, to, z),
            device_id_type=MESH,
        )

    for dx in far_first(NX, 1):
        coupling_copy(dx).start()

    def expansion_copy(d):
        return pltpu.make_async_remote_copy(
            src_ref=expn.at[0, d],
            dst_ref=exp_v.at[d],
            send_sem=e_s.at[d],
            recv_sem=e_r.at[d],
            device_id=at(ahead(d), x, z),
            device_id_type=MESH,
        )

    for d in range(2):
        @pl.when(sends(d))
        def _():
            expansion_copy(d).start()

    def part_of(c):
        return pl.ds(pl.multiple_of(c * rows, rows), rows)

    def dense_copy(k, d, c):
        return pltpu.make_async_remote_copy(
            src_ref=bv.at[k, d, part_of(c), :],
            dst_ref=arr.at[k, d, part_of(c), :],
            send_sem=bv_s.at[k, d, c],
            recv_sem=bv_r.at[k, d, c],
            device_id=at(ahead(d), x, z),
            device_id_type=MESH,
        )

    def partial_copy(k, d, dx):
        to = lax.rem(x + dx, NX)
        return pltpu.make_async_remote_copy(
            src_ref=psend.at[k, d, to],
            dst_ref=prec.at[k, d, x],
            send_sem=p_s.at[k, d, dx],
            recv_sem=p_r.at[k, d, dx],
            device_id=at(ahead(d), to, z),
            device_id_type=MESH,
        )

    def dense(k, d, c0, c1):
        @pl.when(sends(d))
        def _():
            def one(c, carry):
                both = diag_v[d, c].reshape(2 * rows, points)
                field = s_v[d] if k == 0 else v_v[d]
                y = jnp.dot(both, field, preferred_element_type=f32)
                bv[k, d, part_of(c), :] = combine(y).astype(bf16)
                dense_copy(k, d, c).start()
                return carry

            if k == 0:
                for c in range(c0, c1):
                    pltpu.make_async_copy(diag_v.at[d, c], diag_v.at[d, c], dld.at[d, c]).wait()
                    one(c, 0)
            else:
                lax.fori_loop(c0, c1, one, 0)

        if k == 0:
            @pl.when(jnp.logical_not(sends(d)))
            def _():
                for c in range(c0, c1):
                    pltpu.make_async_copy(diag_v.at[d, c], diag_v.at[d, c], dld.at[d, c]).wait()

    def couple(k, d):
        @pl.when(sends(d))
        def _():
            for dz in range(1, NZ):
                gather_copy(k, d, dz).wait_recv()
            y = jnp.dot(cblk[d].reshape(NX * 2 * k_own, kc), ag[k, d], preferred_element_type=f32)
            for to in range(NX):
                psend[k, d, to] = combine(y[to * 2 * k_own : (to + 1) * 2 * k_own]).astype(bf16)
            for dx in far_first(NX, 0):
                partial_copy(k, d, dx).start()

    def arrivals(k, d):
        @pl.when(takes(d))
        def _():
            total = jnp.zeros((k_own, cols), f32)
            for c in range(CHUNKS):
                dense_copy(k, d, c).wait_recv()
                part = pl.ds(c * rows, rows)
                field = s_v[d, part, :].astype(f32) + arr[k, d, part, :].astype(f32)
                total = total + jnp.dot(proj_v[d, :, part], field.astype(bf16), preferred_element_type=f32)
            base[d] = total

    def coupled_sum(k, d):
        for dx in range(NX):
            partial_copy(k, d, dx).wait_recv()
        total = prec[k, d, 0].astype(f32)
        for xx in range(1, NX):
            total = total + prec[k, d, xx].astype(f32)
        coupled = total.astype(bf16)
        cpl[d] = coupled
        return coupled

    def coeffs(k, d):
        @pl.when(takes(d))
        def _():
            coupled = coupled_sum(k - 1, d)
            c = base[d] + jnp.dot(small[d], coupled, preferred_element_type=f32)
            ag[k, d, zrow, :] = c.astype(bf16)

        @pl.when(jnp.logical_not(takes(d)))
        def _():
            ag[k, d, zrow, :] = ag[0, d, zrow, :]

        @pl.when(sends(d))
        def _():
            gather_start(k, d)

    def assemble(k, d, into):
        def one(c, carry):
            part = part_of(c)
            if k == ITERS - 1:
                dense_copy(k, d, c).wait_recv()
            y = jnp.dot(etr[d, part, :], cpl[d], preferred_element_type=f32)
            y = y + arr[k, d, part, :].astype(f32) + s_v[d, part, :].astype(f32)
            into[part, :] = y.astype(bf16)
            return carry

        @pl.when(takes(d))
        def _():
            if k == ITERS - 1:
                coupled_sum(k, d)
            lax.fori_loop(0, CHUNKS, one, 0)

    half = CHUNKS // 2
    dense(0, first, 0, CHUNKS)
    dense(0, second, 0, CHUNKS)
    for d in order:
        @pl.when(takes(d))
        def _():
            expansion_copy(d).wait_recv()
            etr[d] = exp_v[d].astype(f32).T.astype(bf16)
            small[d] = lax.dot_general(
                proj_v[d], exp_v[d], (((1,), (1,)), ((), ())), preferred_element_type=f32
            ).astype(bf16)
    loads[3].wait()
    for dx in range(1, NX):
        coupling_copy(dx).wait_recv()
    couple(0, first)
    couple(0, second)
    for k in range(1, ITERS):
        arrivals(k - 1, first)
        coeffs(k, first)
        assemble(k - 1, first, v_v.at[first])
        dense(k, first, 0, half)
        arrivals(k - 1, second)
        coeffs(k, second)
        dense(k, first, half, CHUNKS)
        assemble(k - 1, second, v_v.at[second])
        dense(k, second, 0, half)
        couple(k, first)
        dense(k, second, half, CHUNKS)
        couple(k, second)
    for d in order:
        assemble(ITERS - 1, d, out.at[d])

        @pl.when(jnp.logical_not(takes(d)))
        def _():
            out[d] = s_v[d]

    for dx in range(1, NX):
        coupling_copy(dx).wait_send()
    for d in range(2):
        @pl.when(sends(d))
        def _():
            expansion_copy(d).wait_send()
            for k in range(ITERS):
                for dz in range(1, NZ):
                    gather_copy(k, d, dz).wait_send()
                for c in range(CHUNKS):
                    dense_copy(k, d, c).wait_send()
                for dx in range(NX):
                    partial_copy(k, d, dx).wait_send()


def write_out(both, out_up, out_dn, sem):
    copies = [
        pltpu.make_async_copy(both.at[d], out.at[0], sem.at[d])
        for d, out in enumerate((out_up, out_dn))
    ]
    for copy in copies:
        copy.start()
    for copy in copies:
        copy.wait()


def shards(source_up, source_down, diag_up, diag_down, projection, expansion, coupling):
    points, cols = source_up.shape[1:]
    k_own = projection.shape[2]
    kc = NZ * k_own
    rows = points // CHUNKS
    bf = jnp.bfloat16
    sem = pltpu.SemaphoreType.DMA
    hbm = pl.BlockSpec(memory_space=pl.ANY)
    vmem = pl.BlockSpec(memory_space=pltpu.VMEM)
    both = pl.pallas_call(
        kernel,
        out_shape=pltpu.VMEM((2, points, cols), bf),
        in_specs=[pl.BlockSpec(memory_space=pltpu.HBM)] * 7,
        out_specs=vmem,
        scratch_shapes=[
            pltpu.VMEM((2, points, cols), bf),
            pltpu.VMEM((2, CHUNKS, 2, rows, points), bf),
            pltpu.VMEM((2, k_own, points), bf),
            pltpu.VMEM((2, k_own, points), bf),
            pltpu.VMEM((2, points, k_own), bf),
            pltpu.VMEM((2, k_own, k_own), bf),
            pltpu.VMEM((2, k_own, cols), jnp.float32),
            pltpu.VMEM((2, NX, 2, k_own, kc), bf),
            pltpu.VMEM((ITERS, 2, kc, cols), bf),
            pltpu.VMEM((ITERS, 2, points, cols), bf),
            pltpu.VMEM((ITERS, 2, points, cols), bf),
            pltpu.VMEM((ITERS, 2, NX, k_own, cols), bf),
            pltpu.VMEM((ITERS, 2, NX, k_own, cols), bf),
            pltpu.VMEM((2, k_own, cols), bf),
            pltpu.VMEM((2, points, cols), bf),
            sem((4,)),
            sem((2, CHUNKS)),
            sem((NX - 1,)),
            sem((NX - 1,)),
            sem((2,)),
            sem((2,)),
            sem((ITERS, 2, NZ - 1)),
            sem((ITERS, 2, NZ - 1)),
            sem((ITERS, 2, CHUNKS)),
            sem((ITERS, 2, CHUNKS)),
            sem((ITERS, 2, NX)),
            sem((ITERS, 2, NX)),
        ],
        compiler_params=pltpu.CompilerParams(
            collective_id=0, has_side_effects=True, vmem_limit_bytes=67043328 - (1 << 20)
        ),
        name="traces",
    )(source_up, source_down, diag_up, diag_down, projection, expansion, coupling)
    return pl.pallas_call(
        write_out,
        out_shape=(
            jax.ShapeDtypeStruct(source_up.shape, bf),
            jax.ShapeDtypeStruct(source_down.shape, bf),
        ),
        in_specs=[vmem],
        out_specs=(hbm, hbm),
        scratch_shapes=[sem((2,))],
        compiler_params=pltpu.CompilerParams(vmem_limit_bytes=4 * 1024 * 1024),
        name="write_out",
    )(both)


def solution(mesh):
    return jax.shard_map(
        shards,
        mesh=mesh,
        in_specs=(
            P("layer", "trace", None),
            P("layer", "trace", None),
            P("layer", None, "trace", None),
            P("layer", None, "trace", None),
            P("layer", None, None, "trace"),
            P("layer", None, None, "trace"),
            P("layer", None, None, "trace", None),
        ),
        out_specs=(P("layer", "trace", None), P("layer", "trace", None)),
        check_vma=False,
    )
```

```python
import jax
import jax.numpy as jnp
from jax import lax
from jax.experimental import pallas as pl
from jax.experimental.pallas import tpu as pltpu
from jax.sharding import PartitionSpec as P

ITERS = 3
NX, NZ = 4, 8
PIECES = 4
CHUNKS = 4
MESH = pl.DeviceIdType.MESH


def combine(stacked):
    rows, half = stacked.shape[0] // 2, stacked.shape[1] // 2
    top, low = stacked[:rows], stacked[rows:]
    return jnp.concatenate([top[:, :half] - low[:, half:], top[:, half:] + low[:, :half]], axis=1)


def kernel(
    src_up, src_dn, dg_up, dg_dn, proj, expn, coup, out,
    s_v, diag_v, proj_v, exp_v, etr, small, base, cblk, ag, bv, arr, psend, prec, v_v,
    ld, dld, c_s, c_r, e_s, e_r, ag_s, ag_r, bv_s, bv_r, p_s, p_r,
):
    g = lax.axis_index("layer")
    t = lax.axis_index("trace")
    layers = lax.axis_size("layer")
    x, z = lax.div(t, NZ), lax.rem(t, NZ)
    points, cols = s_v.shape[1:]
    k_own = proj_v.shape[1]
    kc = NZ * k_own
    rows = points // CHUNKS

    def order_at(k):
        second = lax.rem(g + k, 2)
        return 1 - second, second

    first, second = order = order_at(0)
    f32, bf16 = jnp.float32, jnp.bfloat16

    def at(gg, xx, zz):
        return (gg, xx * NZ + zz)

    def ahead(d):
        return g + 1 - 2 * d

    def sends(d):
        return jnp.logical_and(ahead(d) >= 0, ahead(d) < layers)

    def takes(d):
        behind = g - 1 + 2 * d
        return jnp.logical_and(behind >= 0, behind < layers)

    loads = [
        pltpu.make_async_copy(proj.at[0], proj_v, ld.at[2]),
        pltpu.make_async_copy(src_up.at[0], s_v.at[0], ld.at[0]),
        pltpu.make_async_copy(src_dn.at[0], s_v.at[1], ld.at[1]),
        pltpu.make_async_copy(
            coup.at[0, :, :, :, pl.ds(pl.multiple_of(x * kc, kc), kc)], cblk.at[:, x], ld.at[3]
        ),
    ]
    for copy in loads:
        copy.start()

    barrier = pltpu.get_barrier_semaphore()
    for dz in range(1, NZ):
        pl.semaphore_signal(barrier, inc=1, device_id=at(g, x, lax.rem(z + dz, NZ)), device_id_type=MESH)
    for dx in range(1, NX):
        pl.semaphore_signal(barrier, inc=1, device_id=at(g, lax.rem(x + dx, NX), z), device_id_type=MESH)
    for d in range(2):
        @pl.when(sends(d))
        def _():
            for dx in range(NX):
                pl.semaphore_signal(
                    barrier, inc=1, device_id=at(ahead(d), lax.rem(x + dx, NX), z), device_id_type=MESH
                )

    def diag_load(d, c):
        src = (dg_up, dg_dn)[d]
        return pltpu.make_async_copy(
            src.at[0, :, pl.ds(c * rows, rows), :], diag_v.at[d, c], dld.at[d, c]
        )

    def diag_start(d):
        for c in range(CHUNKS):
            diag_load(d, c).start()

    for copy in loads[:3]:
        copy.wait()
    @pl.when(first == 0)
    def _():
        diag_start(0)
        diag_start(1)

    @pl.when(first == 1)
    def _():
        diag_start(1)
        diag_start(0)

    zrow = pl.ds(pl.multiple_of(z * k_own, k_own), k_own)

    def gather_copy(k, d, dz):
        return pltpu.make_async_remote_copy(
            src_ref=ag.at[k, d, zrow, :],
            dst_ref=ag.at[k, d, zrow, :],
            send_sem=ag_s.at[k, d, dz - 1],
            recv_sem=ag_r.at[k, d, dz - 1],
            device_id=at(g, x, lax.rem(z + dz, NZ)),
            device_id_type=MESH,
        )

    def far_first(count, start):
        return sorted(range(start, count), key=lambda step: -min(step, count - step))

    def gather_start(k, d):
        for dz in far_first(NZ, 1):
            gather_copy(k, d, dz).start()

    def start(d, carry):
        c = jnp.dot(proj_v[d], s_v[d], preferred_element_type=f32)
        ag[0, d, zrow, :] = c.astype(bf16)
        return carry

    lax.fori_loop(0, 2, start, 0)
    field_copies = [pltpu.make_async_copy(s_v.at[d], v_v.at[d], ld.at[4 + d]) for d in range(2)]
    for copy in field_copies:
        copy.start()

    ends = (g > 0).astype(jnp.int32) + (g < layers - 1).astype(jnp.int32)
    pl.semaphore_wait(barrier, NZ - 1 + NX - 1 + NX * ends)

    for d in order:
        @pl.when(sends(d))
        def _():
            gather_start(0, d)

    def coupling_copy(dx):
        to = lax.rem(x + dx, NX)
        return pltpu.make_async_remote_copy(
            src_ref=coup.at[0, :, :, :, pl.ds(pl.multiple_of(to * kc, kc), kc)],
            dst_ref=cblk.at[:, x],
            send_sem=c_s.at[dx - 1],
            recv_sem=c_r.at[dx - 1],
            device_id=at(g, to, z),
            device_id_type=MESH,
        )

    for dx in far_first(NX, 1):
        coupling_copy(dx).start()

    def expansion_copy(d):
        return pltpu.make_async_remote_copy(
            src_ref=expn.at[0, d],
            dst_ref=exp_v.at[d],
            send_sem=e_s.at[d],
            recv_sem=e_r.at[d],
            device_id=at(ahead(d), x, z),
            device_id_type=MESH,
        )

    for d in range(2):
        @pl.when(sends(d))
        def _():
            expansion_copy(d).start()

    def part_of(c):
        return pl.ds(pl.multiple_of(c * rows, rows), rows)

    def dense_copy(k, d, c):
        return pltpu.make_async_remote_copy(
            src_ref=bv.at[k, d, part_of(c), :],
            dst_ref=arr.at[k, d, part_of(c), :],
            send_sem=bv_s.at[k, d, c],
            recv_sem=bv_r.at[k, d, c],
            device_id=at(ahead(d), x, z),
            device_id_type=MESH,
        )

    def partial_copy(k, d, dx):
        to = lax.rem(x + dx, NX)
        return pltpu.make_async_remote_copy(
            src_ref=psend.at[k, d, to],
            dst_ref=prec.at[k, d, x],
            send_sem=p_s.at[k, d, dx],
            recv_sem=p_r.at[k, d, dx],
            device_id=at(ahead(d), to, z),
            device_id_type=MESH,
        )

    def dense(k, d, c0, c1):
        def one(c, carry):
            @pl.when(k == 0)
            def _():
                pltpu.make_async_copy(diag_v.at[d, c], diag_v.at[d, c], dld.at[d, c]).wait()

            @pl.when(sends(d))
            def _():
                both = diag_v[d, c].reshape(2 * rows, points)
                y = jnp.dot(both, v_v[d], preferred_element_type=f32)
                bv[k, d, part_of(c), :] = combine(y).astype(bf16)
                dense_copy(k, d, c).start()

            return carry

        lax.fori_loop(c0, c1, one, 0)

    def couple(k, d):
        @pl.when(sends(d))
        def _():
            for dz in range(1, NZ):
                gather_copy(k, d, dz).wait_recv()
            y = jnp.dot(cblk[d].reshape(NX * 2 * k_own, kc), ag[k, d], preferred_element_type=f32)
            for to in range(NX):
                psend[k, d, to] = combine(y[to * 2 * k_own : (to + 1) * 2 * k_own]).astype(bf16)
            for dx in far_first(NX, 0):
                partial_copy(k, d, dx).start()

    def arrivals(k, d):
        @pl.when(takes(d))
        def _():
            total = jnp.zeros((k_own, cols), f32)
            for c in range(CHUNKS):
                dense_copy(k, d, c).wait_recv()
                part = pl.ds(c * rows, rows)
                field = s_v[d, part, :].astype(f32) + arr[k, d, part, :].astype(f32)
                total = total + jnp.dot(proj_v[d, :, part], field.astype(bf16), preferred_element_type=f32)
            base[d] = total

    def partials_wait(k, d):
        for dx in range(NX):
            partial_copy(k, d, dx).wait_recv()

    def coupled_sum(k, d):
        total = prec[k, d, 0].astype(f32)
        for xx in range(1, NX):
            total = total + prec[k, d, xx].astype(f32)
        return total.astype(bf16)

    def coeffs(k, d):
        @pl.when(takes(d))
        def _():
            partials_wait(k - 1, d)
            stacked = prec[k - 1, d].reshape(NX * k_own, cols)
            c = base[d] + jnp.dot(small[d], stacked, preferred_element_type=f32)
            ag[k, d, zrow, :] = c.astype(bf16)

        @pl.when(jnp.logical_not(takes(d)))
        def _():
            ag[k, d, zrow, :] = ag[0, d, zrow, :]

        @pl.when(sends(d))
        def _():
            gather_start(k, d)

    def assemble(k, d, into):
        def one(c, coupled):
            part = part_of(c)
            y = jnp.dot(etr[d, part, :], coupled, preferred_element_type=f32)
            y = y + arr[k, d, part, :].astype(f32) + s_v[d, part, :].astype(f32)
            into[part, :] = y.astype(bf16)
            return coupled

        lax.fori_loop(0, CHUNKS, one, coupled_sum(k, d))

    def advance(k, d):
        @pl.when(k > 0)
        def _():
            arrivals(k - 1, d)
            coeffs(k, d)

            @pl.when(takes(d))
            def _():
                assemble(k - 1, d, v_v.at[d])

    def iteration(k, carry):
        first, second = order_at(k)
        advance(k, first)
        dense(k, first, 0, CHUNKS)
        advance(k, second)
        dense(k, second, 0, half)

        @pl.when(k == 0)
        def _():
            def expansions(d, carry):
                @pl.when(takes(d))
                def _():
                    expansion_copy(d).wait_recv()
                    etr[d] = exp_v[d].astype(f32).T.astype(bf16)
                    one = lax.dot_general(
                        proj_v[d], exp_v[d], (((1,), (1,)), ((), ())), preferred_element_type=f32
                    )
                    small[d] = jnp.concatenate([one] * NX, axis=1).astype(bf16)

                return carry

            lax.fori_loop(0, 2, expansions, 0)
            loads[3].wait()
            for dx in range(1, NX):
                coupling_copy(dx).wait_recv()

        couple(k, first)
        dense(k, second, half, CHUNKS)
        couple(k, second)
        return carry

    half = CHUNKS // 2
    for copy in field_copies:
        copy.wait()
    lax.fori_loop(0, ITERS, iteration, 0)

    def last(turn, carry):
        d = lax.rem(order_at(ITERS)[0] + turn, 2)

        @pl.when(takes(d))
        def _():
            for c in range(CHUNKS):
                dense_copy(ITERS - 1, d, c).wait_recv()
            partials_wait(ITERS - 1, d)
            assemble(ITERS - 1, d, out.at[d])

        @pl.when(jnp.logical_not(takes(d)))
        def _():
            out[d] = s_v[d]

        return carry

    lax.fori_loop(0, 2, last, 0)

    for dx in range(1, NX):
        coupling_copy(dx).wait_send()

    def sent(d, carry):
        @pl.when(sends(d))
        def _():
            expansion_copy(d).wait_send()

            def sent_in(k, carry):
                for dz in range(1, NZ):
                    gather_copy(k, d, dz).wait_send()
                for c in range(CHUNKS):
                    dense_copy(k, d, c).wait_send()
                for dx in range(NX):
                    partial_copy(k, d, dx).wait_send()
                return carry

            lax.fori_loop(0, ITERS, sent_in, 0)

        return carry

    lax.fori_loop(0, 2, sent, 0)


def write_out(both, out_up, out_dn, sem):
    rows = both.shape[1] // PIECES
    copies = [
        pltpu.make_async_copy(
            both.at[d, pl.ds(i * rows, rows)], out.at[0, pl.ds(i * rows, rows)], sem.at[d, i]
        )
        for d, out in enumerate((out_up, out_dn))
        for i in range(PIECES)
    ]
    for copy in copies:
        copy.start()
    for copy in copies:
        copy.wait()


def shards(source_up, source_down, diag_up, diag_down, projection, expansion, coupling):
    points, cols = source_up.shape[1:]
    k_own = projection.shape[2]
    kc = NZ * k_own
    rows = points // CHUNKS
    bf = jnp.bfloat16
    sem = pltpu.SemaphoreType.DMA
    hbm = pl.BlockSpec(memory_space=pl.ANY)
    vmem = pl.BlockSpec(memory_space=pltpu.VMEM)
    both = pl.pallas_call(
        kernel,
        out_shape=pltpu.VMEM((2, points, cols), bf),
        in_specs=[pl.BlockSpec(memory_space=pltpu.HBM)] * 7,
        out_specs=vmem,
        scratch_shapes=[
            pltpu.VMEM((2, points, cols), bf),
            pltpu.VMEM((2, CHUNKS, 2, rows, points), bf),
            pltpu.VMEM((2, k_own, points), bf),
            pltpu.VMEM((2, k_own, points), bf),
            pltpu.VMEM((2, points, k_own), bf),
            pltpu.VMEM((2, k_own, NX * k_own), bf),
            pltpu.VMEM((2, k_own, cols), jnp.float32),
            pltpu.VMEM((2, NX, 2, k_own, kc), bf),
            pltpu.VMEM((ITERS, 2, kc, cols), bf),
            pltpu.VMEM((ITERS, 2, points, cols), bf),
            pltpu.VMEM((ITERS, 2, points, cols), bf),
            pltpu.VMEM((ITERS, 2, NX, k_own, cols), bf),
            pltpu.VMEM((ITERS, 2, NX, k_own, cols), bf),
            pltpu.VMEM((2, points, cols), bf),
            sem((6,)),
            sem((2, CHUNKS)),
            sem((NX - 1,)),
            sem((NX - 1,)),
            sem((2,)),
            sem((2,)),
            sem((ITERS, 2, NZ - 1)),
            sem((ITERS, 2, NZ - 1)),
            sem((ITERS, 2, CHUNKS)),
            sem((ITERS, 2, CHUNKS)),
            sem((ITERS, 2, NX)),
            sem((ITERS, 2, NX)),
        ],
        compiler_params=pltpu.CompilerParams(
            collective_id=0, has_side_effects=True, vmem_limit_bytes=67043328 - (1 << 20)
        ),
        name="traces",
    )(source_up, source_down, diag_up, diag_down, projection, expansion, coupling)
    return pl.pallas_call(
        write_out,
        out_shape=(
            jax.ShapeDtypeStruct(source_up.shape, bf),
            jax.ShapeDtypeStruct(source_down.shape, bf),
        ),
        in_specs=[vmem],
        out_specs=(hbm, hbm),
        scratch_shapes=[sem((2, PIECES))],
        compiler_params=pltpu.CompilerParams(vmem_limit_bytes=4 * 1024 * 1024),
        name="write_out",
    )(both)


def solution(mesh):
    return jax.shard_map(
        shards,
        mesh=mesh,
        in_specs=(
            P("layer", "trace", None),
            P("layer", "trace", None),
            P("layer", None, "trace", None),
            P("layer", None, "trace", None),
            P("layer", None, None, "trace"),
            P("layer", None, None, "trace"),
            P("layer", None, None, "trace", None),
        ),
        out_specs=(P("layer", "trace", None), P("layer", "trace", None)),
        check_vma=False,
    )
```

```python
import jax
import jax.numpy as jnp
from jax import lax
from jax.experimental import pallas as pl
from jax.experimental.pallas import tpu as pltpu
from jax.sharding import PartitionSpec as P

ITERS = 3
NX, NZ = 4, 8
PIECES = 4
CHUNKS = 4
MESH = pl.DeviceIdType.MESH


def combine(stacked):
    rows, half = stacked.shape[0] // 2, stacked.shape[1] // 2
    top, low = stacked[:rows], stacked[rows:]
    return jnp.concatenate([top[:, :half] - low[:, half:], top[:, half:] + low[:, :half]], axis=1)


def kernel(
    src_up, src_dn, dg_up, dg_dn, proj, expn, coup, out,
    s_v, diag_v, proj_v, exp_v, etr, small, base, cblk, ag, bv, arr, psend, prec, v_v,
    ld, dld, c_s, c_r, e_s, e_r, ag_s, ag_r, bv_s, bv_r, p_s, p_r,
):
    g = lax.axis_index("layer")
    t = lax.axis_index("trace")
    layers = lax.axis_size("layer")
    x, z = lax.div(t, NZ), lax.rem(t, NZ)
    points, cols = s_v.shape[1:]
    k_own = proj_v.shape[1]
    kc = NZ * k_own
    rows = points // CHUNKS

    def order_at(k):
        second = lax.rem(g + k, 2)
        return 1 - second, second

    first, second = order = order_at(0)
    f32, bf16 = jnp.float32, jnp.bfloat16

    def at(gg, xx, zz):
        return (gg, xx * NZ + zz)

    def ahead(d):
        return g + 1 - 2 * d

    def sends(d):
        return jnp.logical_and(ahead(d) >= 0, ahead(d) < layers)

    def takes(d):
        behind = g - 1 + 2 * d
        return jnp.logical_and(behind >= 0, behind < layers)

    loads = [
        pltpu.make_async_copy(proj.at[0], proj_v, ld.at[2]),
        pltpu.make_async_copy(src_up.at[0], s_v.at[0], ld.at[0]),
        pltpu.make_async_copy(src_dn.at[0], s_v.at[1], ld.at[1]),
        pltpu.make_async_copy(
            coup.at[0, :, :, :, pl.ds(pl.multiple_of(x * kc, kc), kc)], cblk.at[:, x], ld.at[3]
        ),
    ]
    for copy in loads:
        copy.start()

    barrier = pltpu.get_barrier_semaphore()
    for dz in range(1, NZ):
        pl.semaphore_signal(barrier, inc=1, device_id=at(g, x, lax.rem(z + dz, NZ)), device_id_type=MESH)
    for dx in range(1, NX):
        pl.semaphore_signal(barrier, inc=1, device_id=at(g, lax.rem(x + dx, NX), z), device_id_type=MESH)
    for d in range(2):
        @pl.when(sends(d))
        def _():
            for dx in range(NX):
                pl.semaphore_signal(
                    barrier, inc=1, device_id=at(ahead(d), lax.rem(x + dx, NX), z), device_id_type=MESH
                )

    def diag_load(d, c):
        src = (dg_up, dg_dn)[d]
        return pltpu.make_async_copy(
            src.at[0, :, pl.ds(c * rows, rows), :], diag_v.at[d, c], dld.at[d, c]
        )

    def diag_start(d):
        for c in range(CHUNKS):
            diag_load(d, c).start()

    for copy in loads[:3]:
        copy.wait()
    @pl.when(first == 0)
    def _():
        diag_start(0)
        diag_start(1)

    @pl.when(first == 1)
    def _():
        diag_start(1)
        diag_start(0)

    zrow = pl.ds(pl.multiple_of(z * k_own, k_own), k_own)

    def gather_copy(k, d, dz):
        return pltpu.make_async_remote_copy(
            src_ref=ag.at[k, d, zrow, :],
            dst_ref=ag.at[k, d, zrow, :],
            send_sem=ag_s.at[k, d, dz - 1],
            recv_sem=ag_r.at[k, d, dz - 1],
            device_id=at(g, x, lax.rem(z + dz, NZ)),
            device_id_type=MESH,
        )

    def far_first(count, start):
        return sorted(range(start, count), key=lambda step: -min(step, count - step))

    def gather_start(k, d):
        for dz in far_first(NZ, 1):
            gather_copy(k, d, dz).start()

    def start(d, carry):
        c = jnp.dot(proj_v[d], s_v[d], preferred_element_type=f32)
        ag[0, d, zrow, :] = c.astype(bf16)
        return carry

    lax.fori_loop(0, 2, start, 0)
    field_copies = [pltpu.make_async_copy(s_v.at[d], v_v.at[d], ld.at[4 + d]) for d in range(2)]
    for copy in field_copies:
        copy.start()

    ends = (g > 0).astype(jnp.int32) + (g < layers - 1).astype(jnp.int32)
    pl.semaphore_wait(barrier, NZ - 1 + NX - 1 + NX * ends)

    for d in order:
        @pl.when(sends(d))
        def _():
            gather_start(0, d)

    def coupling_copy(dx):
        to = lax.rem(x + dx, NX)
        return pltpu.make_async_remote_copy(
            src_ref=coup.at[0, :, :, :, pl.ds(pl.multiple_of(to * kc, kc), kc)],
            dst_ref=cblk.at[:, x],
            send_sem=c_s.at[dx - 1],
            recv_sem=c_r.at[dx - 1],
            device_id=at(g, to, z),
            device_id_type=MESH,
        )

    for dx in far_first(NX, 1):
        coupling_copy(dx).start()

    def expansion_copy(d):
        return pltpu.make_async_remote_copy(
            src_ref=expn.at[0, d],
            dst_ref=exp_v.at[d],
            send_sem=e_s.at[d],
            recv_sem=e_r.at[d],
            device_id=at(ahead(d), x, z),
            device_id_type=MESH,
        )

    for d in range(2):
        @pl.when(sends(d))
        def _():
            expansion_copy(d).start()

    def part_of(c):
        return pl.ds(pl.multiple_of(c * rows, rows), rows)

    def dense_copy(k, d, c):
        return pltpu.make_async_remote_copy(
            src_ref=bv.at[k, d, part_of(c), :],
            dst_ref=arr.at[k, d, part_of(c), :],
            send_sem=bv_s.at[k, d, c],
            recv_sem=bv_r.at[k, d, c],
            device_id=at(ahead(d), x, z),
            device_id_type=MESH,
        )

    def partial_copy(k, d, dx):
        to = lax.rem(x + dx, NX)
        return pltpu.make_async_remote_copy(
            src_ref=psend.at[k, d, to],
            dst_ref=prec.at[k, d, x],
            send_sem=p_s.at[k, d, dx],
            recv_sem=p_r.at[k, d, dx],
            device_id=at(ahead(d), to, z),
            device_id_type=MESH,
        )

    def dense(k, d, c0, c1):
        def one(c, carry):
            @pl.when(k == 0)
            def _():
                pltpu.make_async_copy(diag_v.at[d, c], diag_v.at[d, c], dld.at[d, c]).wait()

            @pl.when(sends(d))
            def _():
                both = diag_v[d, c].reshape(2 * rows, points)
                y = jnp.dot(both, v_v[d], preferred_element_type=f32)
                bv[k, d, part_of(c), :] = combine(y).astype(bf16)
                dense_copy(k, d, c).start()

            return carry

        lax.fori_loop(c0, c1, one, 0)

    def couple(k, d):
        @pl.when(sends(d))
        def _():
            for dz in range(1, NZ):
                gather_copy(k, d, dz).wait_recv()
            y = jnp.dot(cblk[d].reshape(NX * 2 * k_own, kc), ag[k, d], preferred_element_type=f32)
            for to in range(NX):
                psend[k, d, to] = combine(y[to * 2 * k_own : (to + 1) * 2 * k_own]).astype(bf16)
            for dx in far_first(NX, 0):
                partial_copy(k, d, dx).start()

    def arrivals(k, d):
        @pl.when(takes(d))
        def _():
            for c in range(CHUNKS):
                dense_copy(k, d, c).wait_recv()
            field = s_v[d].astype(f32) + arr[k, d].astype(f32)
            base[d] = jnp.dot(proj_v[d], field.astype(bf16), preferred_element_type=f32)

    def partials_wait(k, d):
        for dx in range(NX):
            partial_copy(k, d, dx).wait_recv()

    def coupled_sum(k, d):
        total = prec[k, d, 0].astype(f32)
        for xx in range(1, NX):
            total = total + prec[k, d, xx].astype(f32)
        return total.astype(bf16)

    def coeffs(k, d):
        @pl.when(takes(d))
        def _():
            partials_wait(k - 1, d)
            stacked = prec[k - 1, d].reshape(NX * k_own, cols)
            c = base[d] + jnp.dot(small[d], stacked, preferred_element_type=f32)
            ag[k, d, zrow, :] = c.astype(bf16)

        @pl.when(jnp.logical_not(takes(d)))
        def _():
            ag[k, d, zrow, :] = ag[0, d, zrow, :]

        @pl.when(sends(d))
        def _():
            gather_start(k, d)

    def assemble(k, d, into):
        coupled = coupled_sum(k, d)
        for c in range(1):
            part = pl.ds(c * points // 1, points // 1)
            y = jnp.dot(etr[d, part, :], coupled, preferred_element_type=f32)
            y = y + arr[k, d, part, :].astype(f32) + s_v[d, part, :].astype(f32)
            into[part, :] = y.astype(bf16)

    def renew(k, d):
        @pl.when(k > 0)
        def _():
            arrivals(k - 1, d)
            coeffs(k, d)

    def advance(k, d):
        @pl.when(jnp.logical_and(k > 0, takes(d)))
        def _():
            assemble(k - 1, d, v_v.at[d])

    def iteration(k, carry):
        first, second = order_at(k)
        renew(k, first)
        advance(k, first)
        dense(k, first, 0, half)
        renew(k, second)
        dense(k, first, half, CHUNKS)
        advance(k, second)
        dense(k, second, 0, CHUNKS)

        @pl.when(k == 0)
        def _():
            def expansions(d, carry):
                @pl.when(takes(d))
                def _():
                    expansion_copy(d).wait_recv()
                    etr[d] = exp_v[d].astype(f32).T.astype(bf16)
                    one = lax.dot_general(
                        proj_v[d], exp_v[d], (((1,), (1,)), ((), ())), preferred_element_type=f32
                    )
                    small[d] = jnp.concatenate([one] * NX, axis=1).astype(bf16)

                return carry

            lax.fori_loop(0, 2, expansions, 0)
            loads[3].wait()
            for dx in range(1, NX):
                coupling_copy(dx).wait_recv()

        couple(k, first)
        couple(k, second)
        return carry

    half = CHUNKS // 2
    for copy in field_copies:
        copy.wait()
    lax.fori_loop(0, ITERS, iteration, 0)

    def last(turn, carry):
        d = lax.rem(order_at(ITERS)[0] + turn, 2)

        @pl.when(takes(d))
        def _():
            for c in range(CHUNKS):
                dense_copy(ITERS - 1, d, c).wait_recv()
            partials_wait(ITERS - 1, d)
            assemble(ITERS - 1, d, out.at[d])

        @pl.when(jnp.logical_not(takes(d)))
        def _():
            out[d] = s_v[d]

        return carry

    lax.fori_loop(0, 2, last, 0)

    for dx in range(1, NX):
        coupling_copy(dx).wait_send()

    def sent(d, carry):
        @pl.when(sends(d))
        def _():
            expansion_copy(d).wait_send()

            def sent_in(k, carry):
                for dz in range(1, NZ):
                    gather_copy(k, d, dz).wait_send()
                for c in range(CHUNKS):
                    dense_copy(k, d, c).wait_send()
                for dx in range(NX):
                    partial_copy(k, d, dx).wait_send()
                return carry

            lax.fori_loop(0, ITERS, sent_in, 0)

        return carry

    lax.fori_loop(0, 2, sent, 0)


def write_out(both, out_up, out_dn, sem):
    rows = both.shape[1] // PIECES
    copies = [
        pltpu.make_async_copy(
            both.at[d, pl.ds(i * rows, rows)], out.at[0, pl.ds(i * rows, rows)], sem.at[d, i]
        )
        for d, out in enumerate((out_up, out_dn))
        for i in range(PIECES)
    ]
    for copy in copies:
        copy.start()
    for copy in copies:
        copy.wait()


def shards(source_up, source_down, diag_up, diag_down, projection, expansion, coupling):
    points, cols = source_up.shape[1:]
    k_own = projection.shape[2]
    kc = NZ * k_own
    rows = points // CHUNKS
    bf = jnp.bfloat16
    sem = pltpu.SemaphoreType.DMA
    hbm = pl.BlockSpec(memory_space=pl.ANY)
    vmem = pl.BlockSpec(memory_space=pltpu.VMEM)
    both = pl.pallas_call(
        kernel,
        out_shape=pltpu.VMEM((2, points, cols), bf),
        in_specs=[pl.BlockSpec(memory_space=pltpu.HBM)] * 7,
        out_specs=vmem,
        scratch_shapes=[
            pltpu.VMEM((2, points, cols), bf),
            pltpu.VMEM((2, CHUNKS, 2, rows, points), bf),
            pltpu.VMEM((2, k_own, points), bf),
            pltpu.VMEM((2, k_own, points), bf),
            pltpu.VMEM((2, points, k_own), bf),
            pltpu.VMEM((2, k_own, NX * k_own), bf),
            pltpu.VMEM((2, k_own, cols), jnp.float32),
            pltpu.VMEM((2, NX, 2, k_own, kc), bf),
            pltpu.VMEM((ITERS, 2, kc, cols), bf),
            pltpu.VMEM((ITERS, 2, points, cols), bf),
            pltpu.VMEM((ITERS, 2, points, cols), bf),
            pltpu.VMEM((ITERS, 2, NX, k_own, cols), bf),
            pltpu.VMEM((ITERS, 2, NX, k_own, cols), bf),
            pltpu.VMEM((2, points, cols), bf),
            sem((6,)),
            sem((2, CHUNKS)),
            sem((NX - 1,)),
            sem((NX - 1,)),
            sem((2,)),
            sem((2,)),
            sem((ITERS, 2, NZ - 1)),
            sem((ITERS, 2, NZ - 1)),
            sem((ITERS, 2, CHUNKS)),
            sem((ITERS, 2, CHUNKS)),
            sem((ITERS, 2, NX)),
            sem((ITERS, 2, NX)),
        ],
        compiler_params=pltpu.CompilerParams(
            collective_id=0, has_side_effects=True, vmem_limit_bytes=67043328 - (1 << 20)
        ),
        name="traces",
    )(source_up, source_down, diag_up, diag_down, projection, expansion, coupling)
    return pl.pallas_call(
        write_out,
        out_shape=(
            jax.ShapeDtypeStruct(source_up.shape, bf),
            jax.ShapeDtypeStruct(source_down.shape, bf),
        ),
        in_specs=[vmem],
        out_specs=(hbm, hbm),
        scratch_shapes=[sem((2, PIECES))],
        compiler_params=pltpu.CompilerParams(vmem_limit_bytes=4 * 1024 * 1024),
        name="write_out",
    )(both)


def solution(mesh):
    return jax.shard_map(
        shards,
        mesh=mesh,
        in_specs=(
            P("layer", "trace", None),
            P("layer", "trace", None),
            P("layer", None, "trace", None),
            P("layer", None, "trace", None),
            P("layer", None, None, "trace"),
            P("layer", None, None, "trace"),
            P("layer", None, None, "trace", None),
        ),
        out_specs=(P("layer", "trace", None), P("layer", "trace", None)),
        check_vma=False,
    )
```

```python
import jax
import jax.numpy as jnp
from jax import lax
from jax.experimental import pallas as pl
from jax.experimental.pallas import tpu as pltpu
from jax.sharding import PartitionSpec as P

ITERS = 3
NX, NZ = 4, 8
PIECES = 4
CHUNKS = 2
MESH = pl.DeviceIdType.MESH


def combine(stacked):
    rows, half = stacked.shape[0] // 2, stacked.shape[1] // 2
    top, low = stacked[:rows], stacked[rows:]
    return jnp.concatenate([top[:, :half] - low[:, half:], top[:, half:] + low[:, :half]], axis=1)


def kernel(
    src_up, src_dn, dg_up, dg_dn, proj, expn, coup, out,
    s_v, diag_v, proj_v, exp_v, etr, small, base, cblk, ag, bv, arr, psend, prec, v_v, fixed,
    ld, dld, c_s, c_r, e_s, e_r, ag_s, ag_r, bv_s, bv_r, p_s, p_r,
):
    g = lax.axis_index("layer")
    t = lax.axis_index("trace")
    layers = lax.axis_size("layer")
    x, z = lax.div(t, NZ), lax.rem(t, NZ)
    points, cols = s_v.shape[1:]
    k_own = proj_v.shape[1]
    kc = NZ * k_own
    rows = points // CHUNKS

    def order_at(k):
        second = lax.rem(g + k, 2)
        return 1 - second, second

    first, second = order = order_at(0)
    f32, bf16 = jnp.float32, jnp.bfloat16

    def at(gg, xx, zz):
        return (gg, xx * NZ + zz)

    def ahead(d):
        return g + 1 - 2 * d

    def sends(d):
        return jnp.logical_and(ahead(d) >= 0, ahead(d) < layers)

    def takes(d):
        behind = g - 1 + 2 * d
        return jnp.logical_and(behind >= 0, behind < layers)

    loads = [
        pltpu.make_async_copy(proj.at[0], proj_v, ld.at[2]),
        pltpu.make_async_copy(src_up.at[0], s_v.at[0], ld.at[0]),
        pltpu.make_async_copy(src_dn.at[0], s_v.at[1], ld.at[1]),
        pltpu.make_async_copy(
            coup.at[0, :, :, :, pl.ds(pl.multiple_of(x * kc, kc), kc)], cblk.at[:, x], ld.at[3]
        ),
    ]
    for copy in loads:
        copy.start()

    barrier = pltpu.get_barrier_semaphore()
    for dz in range(1, NZ):
        pl.semaphore_signal(barrier, inc=1, device_id=at(g, x, lax.rem(z + dz, NZ)), device_id_type=MESH)
    for dx in range(1, NX):
        pl.semaphore_signal(barrier, inc=1, device_id=at(g, lax.rem(x + dx, NX), z), device_id_type=MESH)
    for d in range(2):
        @pl.when(sends(d))
        def _():
            for dx in range(NX):
                pl.semaphore_signal(
                    barrier, inc=1, device_id=at(ahead(d), lax.rem(x + dx, NX), z), device_id_type=MESH
                )

    def diag_load(d, c):
        src = (dg_up, dg_dn)[d]
        return pltpu.make_async_copy(
            src.at[0, :, pl.ds(c * rows, rows), :], diag_v.at[d, c], dld.at[d, c]
        )

    def diag_start(d):
        for c in range(CHUNKS):
            diag_load(d, c).start()

    for copy in loads[:3]:
        copy.wait()
    @pl.when(first == 0)
    def _():
        diag_start(0)
        diag_start(1)

    @pl.when(first == 1)
    def _():
        diag_start(1)
        diag_start(0)

    zrow = pl.ds(pl.multiple_of(z * k_own, k_own), k_own)

    def gather_copy(k, d, dz):
        return pltpu.make_async_remote_copy(
            src_ref=ag.at[k, d, zrow, :],
            dst_ref=ag.at[k, d, zrow, :],
            send_sem=ag_s.at[k, d, dz - 1],
            recv_sem=ag_r.at[k, d, dz - 1],
            device_id=at(g, x, lax.rem(z + dz, NZ)),
            device_id_type=MESH,
        )

    def far_first(count, start):
        return sorted(range(start, count), key=lambda step: -min(step, count - step))

    def gather_start(k, d):
        for dz in far_first(NZ, 1):
            gather_copy(k, d, dz).start()

    def start(d, carry):
        c = jnp.dot(proj_v[d], s_v[d], preferred_element_type=f32)
        ag[0, d, zrow, :] = c.astype(bf16)
        return carry

    lax.fori_loop(0, 2, start, 0)
    field_copies = [pltpu.make_async_copy(s_v.at[d], v_v.at[d], ld.at[4 + d]) for d in range(2)]
    for copy in field_copies:
        copy.start()

    ends = (g > 0).astype(jnp.int32) + (g < layers - 1).astype(jnp.int32)
    pl.semaphore_wait(barrier, NZ - 1 + NX - 1 + NX * ends)

    for d in order:
        @pl.when(sends(d))
        def _():
            gather_start(0, d)

    def coupling_copy(dx):
        to = lax.rem(x + dx, NX)
        return pltpu.make_async_remote_copy(
            src_ref=coup.at[0, :, :, :, pl.ds(pl.multiple_of(to * kc, kc), kc)],
            dst_ref=cblk.at[:, x],
            send_sem=c_s.at[dx - 1],
            recv_sem=c_r.at[dx - 1],
            device_id=at(g, to, z),
            device_id_type=MESH,
        )

    for dx in far_first(NX, 1):
        coupling_copy(dx).start()

    def expansion_copy(d):
        return pltpu.make_async_remote_copy(
            src_ref=expn.at[0, d],
            dst_ref=exp_v.at[d],
            send_sem=e_s.at[d],
            recv_sem=e_r.at[d],
            device_id=at(ahead(d), x, z),
            device_id_type=MESH,
        )

    for d in range(2):
        @pl.when(sends(d))
        def _():
            expansion_copy(d).start()

    def part_of(c):
        return pl.ds(pl.multiple_of(c * rows, rows), rows)

    def dense_copy(k, d, c):
        return pltpu.make_async_remote_copy(
            src_ref=bv.at[k, d, part_of(c), :],
            dst_ref=arr.at[k, d, part_of(c), :],
            send_sem=bv_s.at[k, d, c],
            recv_sem=bv_r.at[k, d, c],
            device_id=at(ahead(d), x, z),
            device_id_type=MESH,
        )

    def partial_copy(k, d, dx):
        to = lax.rem(x + dx, NX)
        return pltpu.make_async_remote_copy(
            src_ref=psend.at[k, d, to],
            dst_ref=prec.at[k, d, x],
            send_sem=p_s.at[k, d, dx],
            recv_sem=p_r.at[k, d, dx],
            device_id=at(ahead(d), to, z),
            device_id_type=MESH,
        )

    def dense(k, d, c0, c1):
        def one(c, carry):
            @pl.when(k == 0)
            def _():
                pltpu.make_async_copy(diag_v.at[d, c], diag_v.at[d, c], dld.at[d, c]).wait()

            @pl.when(sends(d))
            def _():
                both = diag_v[d, c].reshape(2 * rows, points)
                y = jnp.dot(both, v_v[d], preferred_element_type=f32)
                bv[k, d, part_of(c), :] = combine(y).astype(bf16)
                dense_copy(k, d, c).start()

            return carry

        lax.fori_loop(c0, c1, one, 0)

    def couple(k, d):
        @pl.when(sends(d))
        def _():
            for dz in range(1, NZ):
                gather_copy(k, d, dz).wait_recv()
            y = jnp.dot(cblk[d].reshape(NX * 2 * k_own, kc), ag[k, d], preferred_element_type=f32)
            for to in range(NX):
                psend[k, d, to] = combine(y[to * 2 * k_own : (to + 1) * 2 * k_own]).astype(bf16)
            for dx in far_first(NX, 0):
                partial_copy(k, d, dx).start()

    def arrivals(k, d):
        @pl.when(takes(d))
        def _():
            for c in range(CHUNKS):
                dense_copy(k, d, c).wait_recv()
            field = s_v[d].astype(f32) + arr[k, d].astype(f32)
            fixed[d] = field
            base[d] = jnp.dot(proj_v[d], field.astype(bf16), preferred_element_type=f32)

    def partials_wait(k, d):
        for dx in range(NX):
            partial_copy(k, d, dx).wait_recv()

    def coupled_sum(k, d):
        total = prec[k, d, 0].astype(f32)
        for xx in range(1, NX):
            total = total + prec[k, d, xx].astype(f32)
        return total.astype(bf16)

    def coeffs(k, d):
        @pl.when(takes(d))
        def _():
            partials_wait(k - 1, d)
            stacked = prec[k - 1, d].reshape(NX * k_own, cols)
            c = base[d] + jnp.dot(small[d], stacked, preferred_element_type=f32)
            ag[k, d, zrow, :] = c.astype(bf16)

        @pl.when(jnp.logical_not(takes(d)))
        def _():
            ag[k, d, zrow, :] = ag[0, d, zrow, :]

        @pl.when(sends(d))
        def _():
            gather_start(k, d)

    def assemble(k, d, into):
        coupled = coupled_sum(k, d)
        for c in range(1):
            part = pl.ds(c * points // 1, points // 1)
            y = jnp.dot(etr[d, part, :], coupled, preferred_element_type=f32)
            into[part, :] = (y + fixed[d, part, :]).astype(bf16)

    def renew(k, d):
        @pl.when(k > 0)
        def _():
            arrivals(k - 1, d)
            coeffs(k, d)

    def advance(k, d):
        @pl.when(jnp.logical_and(k > 0, takes(d)))
        def _():
            assemble(k - 1, d, v_v.at[d])

    def iteration(k, carry):
        first, second = order_at(k)
        renew(k, first)
        advance(k, first)
        dense(k, first, 0, half)
        renew(k, second)
        dense(k, first, half, CHUNKS)
        advance(k, second)
        dense(k, second, 0, CHUNKS)

        @pl.when(k == 0)
        def _():
            def expansions(d, carry):
                @pl.when(takes(d))
                def _():
                    expansion_copy(d).wait_recv()
                    etr[d] = exp_v[d].astype(f32).T.astype(bf16)
                    one = lax.dot_general(
                        proj_v[d], exp_v[d], (((1,), (1,)), ((), ())), preferred_element_type=f32
                    )
                    small[d] = jnp.concatenate([one] * NX, axis=1).astype(bf16)

                return carry

            lax.fori_loop(0, 2, expansions, 0)
            loads[3].wait()
            for dx in range(1, NX):
                coupling_copy(dx).wait_recv()

        couple(k, first)
        couple(k, second)
        return carry

    half = CHUNKS // 2
    for copy in field_copies:
        copy.wait()
    lax.fori_loop(0, ITERS, iteration, 0)

    for dx in range(1, NX):
        coupling_copy(dx).wait_send()

    def sent(d, carry):
        @pl.when(sends(d))
        def _():
            expansion_copy(d).wait_send()

            def sent_in(k, carry):
                for dz in range(1, NZ):
                    gather_copy(k, d, dz).wait_send()
                for c in range(CHUNKS):
                    dense_copy(k, d, c).wait_send()
                for dx in range(NX):
                    partial_copy(k, d, dx).wait_send()
                return carry

            lax.fori_loop(0, ITERS, sent_in, 0)

        return carry

    lax.fori_loop(0, 2, sent, 0)

    def last(turn, carry):
        d = lax.rem(order_at(ITERS)[0] + turn, 2)

        @pl.when(takes(d))
        def _():
            for c in range(CHUNKS):
                dense_copy(ITERS - 1, d, c).wait_recv()
            fixed[d] = s_v[d].astype(f32) + arr[ITERS - 1, d].astype(f32)
            partials_wait(ITERS - 1, d)
            assemble(ITERS - 1, d, out.at[d])

        @pl.when(jnp.logical_not(takes(d)))
        def _():
            out[d] = s_v[d]

        return carry

    lax.fori_loop(0, 2, last, 0)


def write_out(both, out_up, out_dn, sem):
    rows = both.shape[1] // PIECES
    copies = [
        pltpu.make_async_copy(
            both.at[d, pl.ds(i * rows, rows)], out.at[0, pl.ds(i * rows, rows)], sem.at[d, i]
        )
        for d, out in enumerate((out_up, out_dn))
        for i in range(PIECES)
    ]
    for copy in copies:
        copy.start()
    for copy in copies:
        copy.wait()


def shards(source_up, source_down, diag_up, diag_down, projection, expansion, coupling):
    points, cols = source_up.shape[1:]
    k_own = projection.shape[2]
    kc = NZ * k_own
    rows = points // CHUNKS
    bf = jnp.bfloat16
    sem = pltpu.SemaphoreType.DMA
    hbm = pl.BlockSpec(memory_space=pl.ANY)
    vmem = pl.BlockSpec(memory_space=pltpu.VMEM)
    both = pl.pallas_call(
        kernel,
        out_shape=pltpu.VMEM((2, points, cols), bf),
        in_specs=[pl.BlockSpec(memory_space=pltpu.HBM)] * 7,
        out_specs=vmem,
        scratch_shapes=[
            pltpu.VMEM((2, points, cols), bf),
            pltpu.VMEM((2, CHUNKS, 2, rows, points), bf),
            pltpu.VMEM((2, k_own, points), bf),
            pltpu.VMEM((2, k_own, points), bf),
            pltpu.VMEM((2, points, k_own), bf),
            pltpu.VMEM((2, k_own, NX * k_own), bf),
            pltpu.VMEM((2, k_own, cols), jnp.float32),
            pltpu.VMEM((2, NX, 2, k_own, kc), bf),
            pltpu.VMEM((ITERS, 2, kc, cols), bf),
            pltpu.VMEM((ITERS, 2, points, cols), bf),
            pltpu.VMEM((ITERS, 2, points, cols), bf),
            pltpu.VMEM((ITERS, 2, NX, k_own, cols), bf),
            pltpu.VMEM((ITERS, 2, NX, k_own, cols), bf),
            pltpu.VMEM((2, points, cols), bf),
            pltpu.VMEM((2, points, cols), jnp.float32),
            sem((6,)),
            sem((2, CHUNKS)),
            sem((NX - 1,)),
            sem((NX - 1,)),
            sem((2,)),
            sem((2,)),
            sem((ITERS, 2, NZ - 1)),
            sem((ITERS, 2, NZ - 1)),
            sem((ITERS, 2, CHUNKS)),
            sem((ITERS, 2, CHUNKS)),
            sem((ITERS, 2, NX)),
            sem((ITERS, 2, NX)),
        ],
        compiler_params=pltpu.CompilerParams(
            collective_id=0, has_side_effects=True, vmem_limit_bytes=67043328 - (1 << 20)
        ),
        name="traces",
    )(source_up, source_down, diag_up, diag_down, projection, expansion, coupling)
    return pl.pallas_call(
        write_out,
        out_shape=(
            jax.ShapeDtypeStruct(source_up.shape, bf),
            jax.ShapeDtypeStruct(source_down.shape, bf),
        ),
        in_specs=[vmem],
        out_specs=(hbm, hbm),
        scratch_shapes=[sem((2, PIECES))],
        compiler_params=pltpu.CompilerParams(vmem_limit_bytes=4 * 1024 * 1024),
        name="write_out",
    )(both)


def solution(mesh):
    return jax.shard_map(
        shards,
        mesh=mesh,
        in_specs=(
            P("layer", "trace", None),
            P("layer", "trace", None),
            P("layer", None, "trace", None),
            P("layer", None, "trace", None),
            P("layer", None, None, "trace"),
            P("layer", None, None, "trace"),
            P("layer", None, None, "trace", None),
        ),
        out_specs=(P("layer", "trace", None), P("layer", "trace", None)),
        check_vma=False,
    )
```

```python
import jax
import jax.numpy as jnp
from jax import lax
from jax.experimental import pallas as pl
from jax.experimental.pallas import tpu as pltpu
from jax.sharding import PartitionSpec as P

ITERS = 3
NX, NZ = 4, 8
PIECES = 4
CHUNKS = 2
MESH = pl.DeviceIdType.MESH


def combine(stacked):
    rows, half = stacked.shape[0] // 2, stacked.shape[1] // 2
    top, low = stacked[:rows], stacked[rows:]
    return jnp.concatenate([top[:, :half] - low[:, half:], top[:, half:] + low[:, :half]], axis=1)


def kernel(
    src_up, src_dn, dg_up, dg_dn, proj, expn, coup, out,
    s_v, diag_v, proj_v, exp_v, etr, small, base, cblk, ag, bv, arr, psend, prec, v_v, fixed,
    ld, dld, c_s, c_r, e_s, e_r, ag_s, ag_r, bv_s, bv_r, p_s, p_r,
):
    g = lax.axis_index("layer")
    t = lax.axis_index("trace")
    layers = lax.axis_size("layer")
    x, z = lax.div(t, NZ), lax.rem(t, NZ)
    points, cols = s_v.shape[1:]
    k_own = proj_v.shape[1]
    kc = NZ * k_own
    rows = points // CHUNKS

    def order_at(k):
        second = lax.rem(g + k, 2)
        return 1 - second, second

    first, second = order = order_at(0)
    f32, bf16 = jnp.float32, jnp.bfloat16

    def at(gg, xx, zz):
        return (gg, xx * NZ + zz)

    def ahead(d):
        return g + 1 - 2 * d

    def sends(d):
        return jnp.logical_and(ahead(d) >= 0, ahead(d) < layers)

    def takes(d):
        behind = g - 1 + 2 * d
        return jnp.logical_and(behind >= 0, behind < layers)

    loads = [
        pltpu.make_async_copy(proj.at[0], proj_v, ld.at[2]),
        pltpu.make_async_copy(src_up.at[0], s_v.at[0], ld.at[0]),
        pltpu.make_async_copy(src_dn.at[0], s_v.at[1], ld.at[1]),
        pltpu.make_async_copy(
            coup.at[0, :, :, :, pl.ds(pl.multiple_of(x * kc, kc), kc)], cblk.at[:, x], ld.at[3]
        ),
    ]
    for copy in loads:
        copy.start()

    barrier = pltpu.get_barrier_semaphore()
    for dz in range(1, NZ):
        pl.semaphore_signal(barrier, inc=1, device_id=at(g, x, lax.rem(z + dz, NZ)), device_id_type=MESH)
    for dx in range(1, NX):
        pl.semaphore_signal(barrier, inc=1, device_id=at(g, lax.rem(x + dx, NX), z), device_id_type=MESH)
    for d in range(2):
        @pl.when(sends(d))
        def _():
            for dx in range(NX):
                pl.semaphore_signal(
                    barrier, inc=1, device_id=at(ahead(d), lax.rem(x + dx, NX), z), device_id_type=MESH
                )

    def diag_load(d, c):
        src = (dg_up, dg_dn)[d]
        return pltpu.make_async_copy(
            src.at[0, :, pl.ds(c * rows, rows), :], diag_v.at[d, c], dld.at[d, c]
        )

    def diag_start(d):
        for c in range(CHUNKS):
            diag_load(d, c).start()

    for copy in loads[:3]:
        copy.wait()
    @pl.when(first == 0)
    def _():
        diag_start(0)
        diag_start(1)

    @pl.when(first == 1)
    def _():
        diag_start(1)
        diag_start(0)

    zrow = pl.ds(pl.multiple_of(z * k_own, k_own), k_own)

    def gather_copy(k, d, dz):
        return pltpu.make_async_remote_copy(
            src_ref=ag.at[k, d, zrow, :],
            dst_ref=ag.at[k, d, zrow, :],
            send_sem=ag_s.at[k, d, dz - 1],
            recv_sem=ag_r.at[k, d, dz - 1],
            device_id=at(g, x, lax.rem(z + dz, NZ)),
            device_id_type=MESH,
        )

    def far_first(count, start):
        return sorted(range(start, count), key=lambda step: -min(step, count - step))

    def gather_start(k, d):
        for dz in far_first(NZ, 1):
            gather_copy(k, d, dz).start()

    def start(d, carry):
        c = jnp.dot(proj_v[d], s_v[d], preferred_element_type=f32)
        ag[0, d, zrow, :] = c.astype(bf16)
        return carry

    lax.fori_loop(0, 2, start, 0)
    field_copies = [pltpu.make_async_copy(s_v.at[d], v_v.at[d], ld.at[4 + d]) for d in range(2)]
    for copy in field_copies:
        copy.start()

    ends = (g > 0).astype(jnp.int32) + (g < layers - 1).astype(jnp.int32)
    pl.semaphore_wait(barrier, NZ - 1 + NX - 1 + NX * ends)

    for d in order:
        @pl.when(sends(d))
        def _():
            gather_start(0, d)

    def coupling_copy(dx):
        to = lax.rem(x + dx, NX)
        return pltpu.make_async_remote_copy(
            src_ref=coup.at[0, :, :, :, pl.ds(pl.multiple_of(to * kc, kc), kc)],
            dst_ref=cblk.at[:, x],
            send_sem=c_s.at[dx - 1],
            recv_sem=c_r.at[dx - 1],
            device_id=at(g, to, z),
            device_id_type=MESH,
        )

    for dx in far_first(NX, 1):
        coupling_copy(dx).start()

    def expansion_copy(d):
        return pltpu.make_async_remote_copy(
            src_ref=expn.at[0, d],
            dst_ref=exp_v.at[d],
            send_sem=e_s.at[d],
            recv_sem=e_r.at[d],
            device_id=at(ahead(d), x, z),
            device_id_type=MESH,
        )

    for d in range(2):
        @pl.when(sends(d))
        def _():
            expansion_copy(d).start()

    def part_of(c):
        return pl.ds(pl.multiple_of(c * rows, rows), rows)

    def dense_copy(k, d, c):
        return pltpu.make_async_remote_copy(
            src_ref=bv.at[k, d, part_of(c), :],
            dst_ref=arr.at[k, d, part_of(c), :],
            send_sem=bv_s.at[k, d, c],
            recv_sem=bv_r.at[k, d, c],
            device_id=at(ahead(d), x, z),
            device_id_type=MESH,
        )

    def partial_copy(k, d, dx):
        to = lax.rem(x + dx, NX)
        return pltpu.make_async_remote_copy(
            src_ref=psend.at[k, d, to],
            dst_ref=prec.at[k, d, x],
            send_sem=p_s.at[k, d, dx],
            recv_sem=p_r.at[k, d, dx],
            device_id=at(ahead(d), to, z),
            device_id_type=MESH,
        )

    def dense(k, d, c0, c1):
        def one(c, carry):
            @pl.when(k == 0)
            def _():
                pltpu.make_async_copy(diag_v.at[d, c], diag_v.at[d, c], dld.at[d, c]).wait()

            @pl.when(sends(d))
            def _():
                both = diag_v[d, c].reshape(2 * rows, points)
                y = jnp.dot(both, v_v[d], preferred_element_type=f32)
                bv[k, d, part_of(c), :] = combine(y).astype(bf16)
                dense_copy(k, d, c).start()

            return carry

        lax.fori_loop(c0, c1, one, 0)

    def couple(k, d):
        @pl.when(sends(d))
        def _():
            for dz in range(1, NZ):
                gather_copy(k, d, dz).wait_recv()
            y = jnp.dot(cblk[d].reshape(NX * 2 * k_own, kc), ag[k, d], preferred_element_type=f32)
            for to in range(NX):
                psend[k, d, to] = combine(y[to * 2 * k_own : (to + 1) * 2 * k_own]).astype(bf16)
            for dx in far_first(NX, 0):
                partial_copy(k, d, dx).start()

    def arrivals(k, d):
        @pl.when(takes(d))
        def _():
            for c in range(CHUNKS):
                dense_copy(k, d, c).wait_recv()
            field = s_v[d].astype(f32) + arr[k, d].astype(f32)
            fixed[d] = field
            base[d] = jnp.dot(proj_v[d], field.astype(bf16), preferred_element_type=f32)

    def partials_wait(k, d):
        for dx in range(NX):
            partial_copy(k, d, dx).wait_recv()

    def coupled_sum(k, d):
        total = prec[k, d, 0].astype(f32)
        for xx in range(1, NX):
            total = total + prec[k, d, xx].astype(f32)
        return total.astype(bf16)

    def coeffs(k, d):
        @pl.when(takes(d))
        def _():
            partials_wait(k - 1, d)
            stacked = prec[k - 1, d].reshape(NX * k_own, cols)
            c = base[d] + jnp.dot(small[d], stacked, preferred_element_type=f32)
            ag[k, d, zrow, :] = c.astype(bf16)

        @pl.when(jnp.logical_not(takes(d)))
        def _():
            ag[k, d, zrow, :] = ag[0, d, zrow, :]

        @pl.when(sends(d))
        def _():
            gather_start(k, d)

    def assemble(k, d, into):
        coupled = coupled_sum(k, d)
        for c in range(1):
            part = pl.ds(c * points // 1, points // 1)
            y = jnp.dot(etr[d, part, :], coupled, preferred_element_type=f32)
            into[part, :] = (y + fixed[d, part, :]).astype(bf16)

    def renew(k, d):
        @pl.when(k > 0)
        def _():
            arrivals(k - 1, d)
            coeffs(k, d)

    def advance(k, d):
        @pl.when(jnp.logical_and(k > 0, takes(d)))
        def _():
            assemble(k - 1, d, v_v.at[d])

    def iteration(k, carry):
        first, second = order_at(k)
        renew(k, first)
        advance(k, first)
        dense(k, first, 0, half)
        renew(k, second)
        advance(k, second)
        dense(k, first, half, CHUNKS)
        dense(k, second, 0, CHUNKS)

        @pl.when(k == 0)
        def _():
            def expansions(d, carry):
                @pl.when(takes(d))
                def _():
                    expansion_copy(d).wait_recv()
                    etr[d] = exp_v[d].astype(f32).T.astype(bf16)
                    one = lax.dot_general(
                        proj_v[d], exp_v[d], (((1,), (1,)), ((), ())), preferred_element_type=f32
                    )
                    small[d] = jnp.concatenate([one] * NX, axis=1).astype(bf16)

                return carry

            lax.fori_loop(0, 2, expansions, 0)
            loads[3].wait()
            for dx in range(1, NX):
                coupling_copy(dx).wait_recv()

        couple(k, first)
        couple(k, second)
        return carry

    half = CHUNKS // 2
    for copy in field_copies:
        copy.wait()
    lax.fori_loop(0, ITERS, iteration, 0)

    for dx in range(1, NX):
        coupling_copy(dx).wait_send()

    def sent(d, carry):
        @pl.when(sends(d))
        def _():
            expansion_copy(d).wait_send()

            def sent_in(k, carry):
                for dz in range(1, NZ):
                    gather_copy(k, d, dz).wait_send()
                for c in range(CHUNKS):
                    dense_copy(k, d, c).wait_send()
                for dx in range(NX):
                    partial_copy(k, d, dx).wait_send()
                return carry

            lax.fori_loop(0, ITERS, sent_in, 0)

        return carry

    lax.fori_loop(0, 2, sent, 0)

    def last(turn, carry):
        d = lax.rem(order_at(ITERS)[0] + turn, 2)

        @pl.when(takes(d))
        def _():
            for c in range(CHUNKS):
                dense_copy(ITERS - 1, d, c).wait_recv()
            fixed[d] = s_v[d].astype(f32) + arr[ITERS - 1, d].astype(f32)
            partials_wait(ITERS - 1, d)
            assemble(ITERS - 1, d, out.at[d])

        @pl.when(jnp.logical_not(takes(d)))
        def _():
            out[d] = s_v[d]

        return carry

    lax.fori_loop(0, 2, last, 0)


def write_out(both, out_up, out_dn, sem):
    rows = both.shape[1] // PIECES
    copies = [
        pltpu.make_async_copy(
            both.at[d, pl.ds(i * rows, rows)], out.at[0, pl.ds(i * rows, rows)], sem.at[d, i]
        )
        for d, out in enumerate((out_up, out_dn))
        for i in range(PIECES)
    ]
    for copy in copies:
        copy.start()
    for copy in copies:
        copy.wait()


def shards(source_up, source_down, diag_up, diag_down, projection, expansion, coupling):
    points, cols = source_up.shape[1:]
    k_own = projection.shape[2]
    kc = NZ * k_own
    rows = points // CHUNKS
    bf = jnp.bfloat16
    sem = pltpu.SemaphoreType.DMA
    hbm = pl.BlockSpec(memory_space=pl.ANY)
    vmem = pl.BlockSpec(memory_space=pltpu.VMEM)
    both = pl.pallas_call(
        kernel,
        out_shape=pltpu.VMEM((2, points, cols), bf),
        in_specs=[pl.BlockSpec(memory_space=pltpu.HBM)] * 7,
        out_specs=vmem,
        scratch_shapes=[
            pltpu.VMEM((2, points, cols), bf),
            pltpu.VMEM((2, CHUNKS, 2, rows, points), bf),
            pltpu.VMEM((2, k_own, points), bf),
            pltpu.VMEM((2, k_own, points), bf),
            pltpu.VMEM((2, points, k_own), bf),
            pltpu.VMEM((2, k_own, NX * k_own), bf),
            pltpu.VMEM((2, k_own, cols), jnp.float32),
            pltpu.VMEM((2, NX, 2, k_own, kc), bf),
            pltpu.VMEM((ITERS, 2, kc, cols), bf),
            pltpu.VMEM((ITERS, 2, points, cols), bf),
            pltpu.VMEM((ITERS, 2, points, cols), bf),
            pltpu.VMEM((ITERS, 2, NX, k_own, cols), bf),
            pltpu.VMEM((ITERS, 2, NX, k_own, cols), bf),
            pltpu.VMEM((2, points, cols), bf),
            pltpu.VMEM((2, points, cols), jnp.float32),
            sem((6,)),
            sem((2, CHUNKS)),
            sem((NX - 1,)),
            sem((NX - 1,)),
            sem((2,)),
            sem((2,)),
            sem((ITERS, 2, NZ - 1)),
            sem((ITERS, 2, NZ - 1)),
            sem((ITERS, 2, CHUNKS)),
            sem((ITERS, 2, CHUNKS)),
            sem((ITERS, 2, NX)),
            sem((ITERS, 2, NX)),
        ],
        compiler_params=pltpu.CompilerParams(
            collective_id=0, has_side_effects=True, vmem_limit_bytes=67043328 - (1 << 20)
        ),
        name="traces",
    )(source_up, source_down, diag_up, diag_down, projection, expansion, coupling)
    return pl.pallas_call(
        write_out,
        out_shape=(
            jax.ShapeDtypeStruct(source_up.shape, bf),
            jax.ShapeDtypeStruct(source_down.shape, bf),
        ),
        in_specs=[vmem],
        out_specs=(hbm, hbm),
        scratch_shapes=[sem((2, PIECES))],
        compiler_params=pltpu.CompilerParams(vmem_limit_bytes=4 * 1024 * 1024),
        name="write_out",
    )(both)


def solution(mesh):
    return jax.shard_map(
        shards,
        mesh=mesh,
        in_specs=(
            P("layer", "trace", None),
            P("layer", "trace", None),
            P("layer", None, "trace", None),
            P("layer", None, "trace", None),
            P("layer", None, None, "trace"),
            P("layer", None, None, "trace"),
            P("layer", None, None, "trace", None),
        ),
        out_specs=(P("layer", "trace", None), P("layer", "trace", None)),
        check_vma=False,
    )
```
